128 devices in a mesh: gx: 8 (over x, core), gy: 16 (over y, z).
Axes of the slice: x: 4, y: 4, z: 4, core: 2. Of those that a mesh axis runs over, the one named last changes fastest.
Arguments:
- state: float32 [1024, 2, 128, 128], P(('gx', 'gy')), may hold values from -6 to 6
- hamiltonian: float32 [2, 128, 128], replicated, may hold values from -0.5 to 0.5
- couplings: float32 [16, 128, 128], replicated, may hold values from -0.125 to 0.125
- bath_coef: float32 [2, 16], replicated, may hold values from 0.2 to 1
- bath_rate: float32 [16], replicated, may hold values from 0.02 to 0.2
- occupation: int32 [1024, 16], P(('gx', 'gy')), may hold values from 0 to 5
- send_list: int32 [128, 128, 1], P(('gx', 'gy')), may hold values from -1 to 7
- up_index: int32 [1024, 16], P(('gx', 'gy')), may hold values from -1 to 135
- down_index: int32 [1024, 16], P(('gx', 'gy')), may hold values from -1 to 135
- step: float32 [1], replicated, may hold values from 0.5 to 1.5
Outputs:
- derivative: float32 [1024, 2, 128, 128], P(('gx', 'gy'))
- advanced: float32 [1024, 2, 128, 128], P(('gx', 'gy'))
The draws below stay inside these ranges and needn't reach their ends.
All inputs are finite; a program needn't handle non-finite values.
Results may differ from the reference program's by a relative error of at most 0.0003.
Values sent between devices are 32-bit elements; how exact they have to be, the bound alone decides.
No kernel may reach another device: no remote copies, remote signals or barrier semaphores. Data moves between devices by JAX's collectives and lax.ppermute only.
A program may use at most 256 MiB of HBM per device.

```python
import math
import jax
import jax.numpy as jnp
from jax import lax

NS = 128
K = 16
M_DEV = 8
S = 1
TOTAL = 1024


def draw_occupation(key, part):
    devices = TOTAL // M_DEV
    owner = jnp.arange(TOTAL, dtype=jnp.int32) // M_DEV
    highest = jnp.minimum(1 + 5 * owner // max(devices - 1, 1), 5)
    tops = jnp.broadcast_to((highest + 1)[:, None], (TOTAL, K))
    values = jax.random.randint(jax.random.fold_in(key, 11), (TOTAL, K), 0, 6)
    values = jnp.minimum(values, tops - 1)
    return values.at[TOTAL - 1, 0].set(5).astype(jnp.int32)


def draw_send_list(key, part):
    devices = TOTAL // M_DEV
    values = jax.random.randint(jax.random.fold_in(key, 21), (devices, devices, S), 0, M_DEV)
    keep = jax.random.randint(jax.random.fold_in(key, 22), (devices, devices, S), 0, 10) < 7
    values = jnp.where(keep, values, -1)
    values = values.at[0, 0, 0].set(M_DEV - 1).at[0, 1, 0].set(-1)
    return values.astype(jnp.int32)


def neighbour_draw(key, salt):
    devices = TOTAL // M_DEV
    kind = jax.random.randint(jax.random.fold_in(key, salt), (TOTAL, K), 0, 10)
    local = jax.random.randint(jax.random.fold_in(key, salt + 1), (TOTAL, K), 0, M_DEV)
    remote = M_DEV + jax.random.randint(jax.random.fold_in(key, salt + 2), (TOTAL, K), 0, devices * S)
    values = jnp.where(kind < 1, -1, jnp.where(kind < 5, local, remote))
    values = values.at[0, 0].set(M_DEV + devices * S - 1).at[0, 1].set(-1)
    return values.astype(jnp.int32)


def draw_up_index(key, part):
    return neighbour_draw(key, 31)


def draw_down_index(key, part):
    return neighbour_draw(key, 41)


def steps_of(stream_key, extent, pieces, smallest, high):
    gain = 1.0
    for dim, shards_of in pieces:
        steps = jax.random.uniform(jax.random.fold_in(jax.random.fold_in(stream_key, 6), dim), (shards_of,), jnp.float32, smallest / len(pieces), high / len(pieces))
        gain = gain * jnp.repeat(jnp.exp(steps), extent[dim] // shards_of).reshape((-1,) + (1,) * (len(extent) - 1 - dim))
    return gain


def gaussian(stream_key, extent, spread, bound, pieces=(), kind=jnp.bfloat16):
    gain = steps_of(stream_key, extent, pieces, -0.22, 0.18) if pieces else 1.0
    result = jax.random.normal(stream_key, extent, jnp.float32) * spread * gain
    return jnp.minimum(jnp.maximum(result, -bound), bound).astype(kind)


def setup_inputs(seed: int = 0) -> dict:
    splits = jax.random.split(jax.random.key(seed), 11)
    return {
        "state": gaussian(splits[0], (TOTAL, 2, NS, NS), 1.0, 6.0, ((0, 128),), jnp.float32),
        "hamiltonian": gaussian(splits[1], (2, NS, NS), NS ** -0.5, 0.5, (), jnp.float32),
        "couplings": gaussian(splits[2], (K, NS, NS), (NS * K) ** -0.5, 0.125, (), jnp.float32),
        "bath_coef": jnp.clip(jax.random.uniform(splits[3], (2, K), jnp.float32, 0.2, 1.0), 0.2, 1.0),
        "bath_rate": jnp.clip(jnp.exp(jax.random.uniform(splits[4], (K,), jnp.float32, math.log(0.02), math.log(0.2))), 0.02, 0.2),
        "occupation": draw_occupation(jax.random.fold_in(splits[10], 71), 0),
        "send_list": draw_send_list(jax.random.fold_in(splits[10], 71), 0),
        "up_index": draw_up_index(jax.random.fold_in(splits[10], 71), 0),
        "down_index": draw_down_index(jax.random.fold_in(splits[10], 71), 0),
        "step": jnp.clip(jax.random.uniform(splits[9], (1,), jnp.float32, 0.5, 1.5), 0.5, 1.5),
    }


def left_product(matrix, rows):
    return jnp.einsum('ij,mcjl->mcil', matrix, rows, precision=lax.Precision.HIGHEST)

def right_product(rows, matrix):
    return jnp.einsum('mcij,jl->mcil', rows, matrix, precision=lax.Precision.HIGHEST)

def derive(local, buffer, occupation, up_index, down_index, hamiltonian, couplings, bath_coef, bath_rate):
    counts = occupation.astype(local.dtype)
    modes = couplings.shape[0]
    rows = local.shape[0]
    joined = jnp.concatenate([up_index, down_index], axis=1).T.reshape(-1)
    picked = jnp.take(buffer, jnp.clip(joined, 0, buffer.shape[0] - 1).astype(jnp.int32), axis=0)
    picked = picked * (joined >= 0).astype(buffer.dtype)[:, None, None, None]
    picked = picked.reshape((2 * modes, rows) + local.shape[1:])
    stacked = jnp.concatenate([couplings, couplings], axis=0)
    lefts = jnp.einsum('kij,kmcjl->kmcil', stacked, picked, precision=lax.Precision.HIGHEST)
    rights = jnp.einsum('kmcij,kjl->kmcil', picked, stacked, precision=lax.Precision.HIGHEST)
    comm = lax.optimization_barrier(jnp.sum(lefts[:modes] - rights[:modes], axis=0))
    left_low, right_low = (lefts[modes:], rights[modes:])
    coef_real = bath_coef[0][:, None, None, None]
    coef_imag = bath_coef[1][:, None, None, None]
    part_x = coef_real * (left_low[:, :, 0] - right_low[:, :, 0]) - coef_imag * (left_low[:, :, 1] + right_low[:, :, 1])
    part_y = coef_real * (left_low[:, :, 1] - right_low[:, :, 1]) + coef_imag * (left_low[:, :, 0] + right_low[:, :, 0])
    weight = counts.T[:, :, None, None]
    sum_x = lax.optimization_barrier(jnp.sum(weight * part_x, axis=0))
    sum_y = lax.optimization_barrier(jnp.sum(weight * part_y, axis=0))
    total = jnp.stack([comm[:, 1] + sum_y, -comm[:, 0] - sum_x], axis=1)
    ham_real, ham_imag = (hamiltonian[0], hamiltonian[1])
    real_part, imag_part = (local[:, 0:1], local[:, 1:2])
    left_real = left_product(ham_real, real_part) - left_product(ham_imag, imag_part)
    left_imag = left_product(ham_real, imag_part) + left_product(ham_imag, real_part)
    right_real = right_product(real_part, ham_real) - right_product(imag_part, ham_imag)
    right_imag = right_product(real_part, ham_imag) + right_product(imag_part, ham_real)
    comm_real = left_real - right_real
    comm_imag = left_imag - right_imag
    total = total + jnp.concatenate([comm_imag, -comm_real], axis=1)
    damping = lax.optimization_barrier(jnp.sum(counts * bath_rate[None, :], axis=1))
    return total - damping[:, None, None, None] * local

def reference(state, hamiltonian, couplings, bath_coef, bath_rate, occupation, send_list, up_index, down_index, step):
    devices = TOTAL // M_DEV

    def one_device(dev):
        local = lax.dynamic_slice_in_dim(state, dev * M_DEV, M_DEV, 0)
        chosen = lax.dynamic_index_in_dim(send_list, dev, 1, keepdims=False)
        owners = jnp.arange(devices, dtype=jnp.int32)[:, None]
        flat = owners * M_DEV + jnp.clip(chosen, 0, M_DEV - 1).astype(jnp.int32)
        arrived = jnp.take(state, flat.reshape(-1), axis=0)
        arrived = arrived * (chosen.reshape(-1) >= 0).astype(state.dtype)[:, None, None, None]
        buffer = jnp.concatenate([local, arrived], axis=0)
        occ = lax.dynamic_slice_in_dim(occupation, dev * M_DEV, M_DEV, 0)
        ups = lax.dynamic_slice_in_dim(up_index, dev * M_DEV, M_DEV, 0)
        downs = lax.dynamic_slice_in_dim(down_index, dev * M_DEV, M_DEV, 0)
        return derive(local, buffer, occ, ups, downs, hamiltonian, couplings, bath_coef, bath_rate)
    parts = lax.map(one_device, jnp.arange(devices, dtype=jnp.int32))
    derivative = parts.reshape(state.shape)
    count = TOTAL * 2 * NS * NS
    rms = jnp.sqrt(jnp.sum(derivative * derivative) / count + 1e-06)
    advanced = state + step[0] / rms * derivative
    return (derivative, advanced)
```

```python
import functools

import jax
import jax.numpy as jnp
from jax import lax
from jax.experimental import pallas as pl
from jax.experimental.pallas import tpu as pltpu
from jax.sharding import Mesh
from jax.sharding import PartitionSpec as P

PLANE = ("gy_0", "gy_1")
LINE = ("gx_0", "gx_1")
ALL = LINE + PLANE
UNROLL = 4
F32 = jnp.float32
BF16 = jnp.bfloat16


def dot(a, b):
    return jnp.dot(a, b, preferred_element_type=F32)


def split(value):
    high = value.astype(BF16)
    return high, (value - high.astype(F32)).astype(BF16)


def load_mode(q_ref, k, rows_ref, cols_ref):
    high, low = split(q_ref[k])
    n = high.shape[0]
    rows_ref[k, :n] = high
    rows_ref[k, n:] = low
    cols_ref[k, :, :n] = high
    cols_ref[k, :, n:] = low


def products(q_rows, q_cols, u):
    n = u.shape[-1]
    high, low = split(u)
    q_high = q_rows[:n]
    wide_high = jnp.concatenate([high[0], high[1]], axis=1)
    wide_low = jnp.concatenate([low[0], low[1]], axis=1)
    z = dot(q_rows, wide_high)
    left = z[:n] + z[n:] + dot(q_high, wide_low)
    tall_high = high.reshape(2 * n, n)
    tall_low = low.reshape(2 * n, n)
    w = dot(tall_high, q_cols)
    right = w[:, :n] + w[:, n:] + dot(tall_low, q_high)
    return left[:, :n], left[:, n:], right[:n], right[n:]


def compact_kernel(table_ref, list_ref, count_ref):
    slots = table_ref.shape[0]

    def visit(i, count):
        source = table_ref[i]
        list_ref[count] = i * 128 + source
        return count + (source >= 0).astype(jnp.int32)

    count = lax.fori_loop(0, slots, visit, jnp.int32(0), unroll=8)
    for i in range(UNROLL):
        list_ref[count + i] = 0
    count_ref[0] = count


def compact(table):
    slots = table.shape[0]
    smem = pl.BlockSpec(memory_space=pltpu.SMEM)
    return pl.pallas_call(
        compact_kernel,
        out_shape=(
            jax.ShapeDtypeStruct((slots + UNROLL,), jnp.int32),
            jax.ShapeDtypeStruct((1,), jnp.int32),
        ),
        in_specs=[smem],
        out_specs=(smem, smem),
    )(table)


def add_terms(list_ref, count_ref, occ_ref, coef_ref, source_ref, rows_ref, cols_ref, out_ref):
    modes = rows_ref.shape[0]
    count = count_ref[0]

    def step(i, carry):
        for j in range(UNROLL):
            t = i * UNROLL + j
            code = list_ref[t]
            slot = code >> 7
            m = slot // (2 * modes)
            down = (slot // modes) % 2
            k = slot % modes
            weight = occ_ref[m * modes + k].astype(F32)
            live = t < count
            alpha = jnp.where(down == 1, weight * coef_ref[k], 1.0)
            beta = jnp.where(down == 1, weight * coef_ref[modes + k], 0.0)
            alpha = jnp.where(live, alpha, 0.0)
            beta = jnp.where(live, beta, 0.0)
            a_re, a_im, b_re, b_im = products(rows_ref[k], cols_ref[k], source_ref[code & 127])
            out_ref[m, 0] += alpha * (a_im - b_im) + beta * (a_re + b_re)
            out_ref[m, 1] += beta * (a_im + b_im) - alpha * (a_re - b_re)
        return carry

    lax.fori_loop(0, (count + UNROLL - 1) // UNROLL, step, 0)


def own_kernel(
    list_ref, count_ref, occ_ref, coef_ref, damp_ref, source_ref, q_ref, h_ref, out_ref, rows_ref, cols_ref,
    hrows_ref, hcols_ref
):
    for k in range(q_ref.shape[0]):
        load_mode(q_ref, k, rows_ref, cols_ref)
    for k in range(2):
        load_mode(h_ref, k, hrows_ref, hcols_ref)

    def one(m, carry):
        u = source_ref[m]
        ra, ia, rb, ib = products(hrows_ref[0], hcols_ref[0], u)
        rc, ic, rd, idd = products(hrows_ref[1], hcols_ref[1], u)
        comm_re = (ra - ic) - (rb - idd)
        comm_im = (ia + rc) - (ib + rd)
        out_ref[m, 0] = comm_im - damp_ref[m] * u[0]
        out_ref[m, 1] = -comm_re - damp_ref[m] * u[1]
        return carry

    lax.fori_loop(0, source_ref.shape[0], one, 0)
    add_terms(list_ref, count_ref, occ_ref, coef_ref, source_ref, rows_ref, cols_ref, out_ref)


def far_kernel(list_ref, count_ref, occ_ref, coef_ref, source_ref, q_ref, out_ref, rows_ref, cols_ref):
    for k in range(q_ref.shape[0]):
        load_mode(q_ref, k, rows_ref, cols_ref)

    def clear(m, carry):
        out_ref[m] = jnp.zeros(out_ref.shape[1:], F32)
        return carry

    lax.fori_loop(0, out_ref.shape[0], clear, 0)
    add_terms(list_ref, count_ref, occ_ref, coef_ref, source_ref, rows_ref, cols_ref, out_ref)


def call(kernel, scalars, arrays, dests, scratch):
    smem = pl.BlockSpec(memory_space=pltpu.SMEM)
    vmem = pl.BlockSpec(memory_space=pltpu.VMEM)
    n = arrays[0].shape[-1]
    return pl.pallas_call(
        kernel,
        out_shape=jax.ShapeDtypeStruct((dests, 2, n, n), F32),
        in_specs=[smem] * len(scalars) + [vmem] * len(arrays),
        out_specs=vmem,
        scratch_shapes=scratch,
        compiler_params=pltpu.CompilerParams(vmem_limit_bytes=48 << 20),
    )(*scalars, *arrays)


def body(
    state,
    hamiltonian,
    couplings,
    bath_coef,
    bath_rate,
    occupation,
    send_list,
    up_index,
    down_index,
    step,
):
    local, _, n, _ = state.shape
    modes = couplings.shape[0]
    nx, nc = lax.axis_size("gx_0"), lax.axis_size("gx_1")
    line, plane = nx * nc, lax.axis_size("gy_0") * lax.axis_size("gy_1")
    x, c = lax.axis_index("gx_0"), lax.axis_index("gx_1")
    me = x * nc + c
    q = lax.axis_index("gy_0") * lax.axis_size("gy_1") + lax.axis_index("gy_1")

    gathered = lax.all_gather(state, PLANE, axis=0, tiled=True)

    mine = jnp.stack([up_index, down_index, occupation])
    tables = lax.all_to_all(
        jnp.broadcast_to(mine, (line,) + mine.shape), LINE, split_axis=0, concat_axis=0, tiled=True
    )
    listed = send_list.reshape(line, plane).T
    listed = lax.all_to_all(listed, PLANE, split_axis=0, concat_axis=0, tiled=True)

    offset = jnp.arange(line, dtype=jnp.int32)
    dest = (x + offset % nx) % nx * nc + (c + offset // nx) % nc
    pick = (dest[:, None] == jnp.arange(line, dtype=jnp.int32)[None, :]).astype(jnp.int32)
    tables = jnp.sum(pick[:, :, None, None, None] * tables[None], axis=1)
    listed = jnp.sum(pick[None, :, :] * listed[:, None, :], axis=2)
    entry = jnp.transpose(tables[:, :2], (0, 2, 1, 3)).reshape(line, local * 2 * modes)
    occ = tables[:, 2].reshape(line, local * modes)
    far = entry - local
    far_plane = far % plane
    hit = far_plane[:, :, None] == jnp.arange(plane, dtype=jnp.int32)
    slot = jnp.sum(hit * listed.T[:, None, :], axis=2)
    good = (far >= 0) & (far // plane == me) & (slot >= 0)
    table = jnp.where(good, far_plane * local + slot, -1).reshape(2, -1)
    occ = occ.reshape(2, -1)

    coef = bath_coef.reshape(-1)
    damp = jnp.sum(occupation.astype(F32) * bath_rate[None, :], axis=1)
    near = jnp.stack([up_index, down_index], axis=1).reshape(-1)
    near = jnp.where(near < local, near, -1)
    near_list, near_count = compact(near)

    mode_scratch = [pltpu.VMEM((modes, 2 * n, n), BF16), pltpu.VMEM((modes, n, 2 * n), BF16)]
    ham_scratch = [pltpu.VMEM((2, 2 * n, n), BF16), pltpu.VMEM((2, n, 2 * n), BF16)]
    own = call(
        own_kernel,
        [near_list, near_count, occupation.reshape(-1), coef, damp],
        [state, couplings, hamiltonian],
        local,
        mode_scratch + ham_scratch,
    )
    other_list, other_count = compact(table[1])
    same_list, same_count = compact(table[0])

    swap = call(
        far_kernel, [other_list, other_count, occ[1], coef], [gathered, couplings], nx * local, mode_scratch
    )
    swapped = lax.ppermute(swap, "gx_1", [(i, (i + 1) % nc) for i in range(nc)])
    same = call(
        far_kernel, [same_list, same_count, occ[0], coef], [gathered, couplings], nx * local, mode_scratch
    )
    pieces = [
        same[d * local : (d + 1) * local] + swapped[d * local : (d + 1) * local] for d in range(nx)
    ]
    derivative = own + pieces[0]
    for d in (2, 1, 3):
        derivative = derivative + lax.ppermute(pieces[d], "gx_0", [(i, (i + d) % nx) for i in range(nx)])

    total = jnp.sum(derivative * derivative)
    for axis in ALL:
        size = lax.axis_size(axis)
        parts = [
            lax.ppermute(total, axis, [(i, (i + d) % size) for i in range(size)]) for d in range(1, size)
        ]
        total = functools.reduce(jnp.add, parts, total)
    count = local * line * plane * 2 * n * n
    rms = jnp.sqrt(total / count + 1e-06)
    return derivative, state + step[0] / rms * derivative


def solution(mesh):
    torus = Mesh(mesh.devices.reshape(4, 2, 4, 4), ("gx_0", "gx_1", "gy_0", "gy_1"))
    whole = P(ALL, None, None, None)
    index = P(ALL, None)
    in_specs = (whole, P(), P(), P(), P(), index, P(ALL, None, None), index, index, P())
    return jax.shard_map(body, mesh=torus, in_specs=in_specs, out_specs=(whole, whole), check_vma=False)
```

```python
import functools

import jax
import jax.numpy as jnp
import numpy as np
from jax import lax
from jax.experimental import pallas as pl
from jax.experimental.pallas import tpu as pltpu
from jax.sharding import Mesh
from jax.sharding import PartitionSpec as P

ALL = ("xh", "xl", "c", "yh", "yl", "zh", "zl")
UNROLL = 4
F32 = jnp.float32
BF16 = jnp.bfloat16
PARTS = ((0, 3, "xyz"), (3, 6, "yzx"), (6, 8, "zxy"))


def dot(a, b):
    return jnp.dot(a, b, preferred_element_type=F32)


def cell_pairs(axis):
    pairs = []
    for x, c, y, z in np.ndindex(4, 2, 4, 4):
        at = {"x": x, "y": y, "z": z}
        to = dict(at)
        to[axis] = (((at[axis] + c) % 4 ^ 1) - c) % 4
        pairs.append((((x * 2 + c) * 4 + y) * 4 + z, ((to["x"] * 2 + c) * 4 + to["y"]) * 4 + to["z"]))
    return pairs


def flip(value, axis):
    return lax.ppermute(value, axis, [(0, 1), (1, 0)])


def split(value):
    high = value.astype(BF16)
    return high, (value - high.astype(F32)).astype(BF16)


def load_modes(q_ref, left_ref, right_ref):
    n = q_ref.shape[-1]

    def one(k, carry):
        high, low = split(q_ref[k])
        left_ref[k, :n, :n] = high
        left_ref[k, :n, n:] = high
        left_ref[k, n:, :n] = low
        left_ref[k, n:, n:] = low
        right_ref[k, :n, :n] = high
        right_ref[k, :n, n:] = low
        right_ref[k, n:, :n] = high
        right_ref[k, n:, n:] = low
        return carry

    lax.fori_loop(0, q_ref.shape[0], one, 0)


def products(left, right, u):
    n = u.shape[-1]
    high, low = split(u)
    tall = jnp.concatenate(
        [jnp.concatenate([high[0], high[1]], axis=1), jnp.concatenate([low[0], low[1]], axis=1)], axis=0
    )
    z = dot(left, tall)
    z = z[:n] + z[n:]
    wide = jnp.concatenate([high.reshape(2 * n, n), low.reshape(2 * n, n)], axis=1)
    w = dot(wide, right)
    w = w[:, :n] + w[:, n:]
    return z[:, :n], z[:, n:], w[:n], w[n:]


def plan_kernel(at_ref, low_ref, high_ref, lists_ref, plan_ref):
    x, y, z, c = (at_ref[i] for i in range(4))
    table = jnp.concatenate([low_ref[...], high_ref[...]], axis=0)
    row = lax.broadcasted_iota(jnp.int32, table.shape, 0) >> 3
    lane = lax.broadcasted_iota(jnp.int32, table.shape, 1)
    dx, dy, dz = x ^ (row & 2), y ^ ((row & 4) >> 1), z ^ ((row & 8) >> 2)
    device = (((dx << 1) + (c ^ (row & 1)) << 2) + dy << 2) + dz
    chosen = jnp.where(lane == device, 1.0, 0.0)
    listed = lax.dot_general(
        chosen, lists_ref[...], (((1,), (1,)), ((), ())), preferred_element_type=F32
    )
    far = table - 8
    owner = {"x": far >> 5, "y": (far >> 2) & 3, "z": far & 3}
    inside = (far >= 0) & (((far >> 4) & 1) == c) & (lane < 32)
    differs = {}
    for a, ours in zip("xyz", (x, y, z)):
        theirs, ours = (owner[a] + c) & 3, (ours + c) & 3
        inside = inside & ((theirs >> 1) == (ours >> 1))
        differs[a] = (theirs ^ ours) & 1
    member = sum(differs[a] << s for s, a in enumerate(PARTS[2][2]))
    slot = jnp.full(table.shape, -1.0, F32)
    for b in range(8):
        slot = jnp.where(member == b, listed[:, b : b + 1], slot)
    slot = slot.astype(jnp.int32)
    position = jnp.zeros(table.shape, jnp.int32)
    for lo, hi, order in PARTS:
        block = sum(differs[a] << s for s, a in enumerate(order))
        position = jnp.where((slot >= lo) & (slot < hi), 8 * lo + block * (hi - lo) + slot - lo, position)
    valid = inside & (slot >= 0)
    power = (1 << (lane & 15)).astype(F32)

    def half(bits):
        return jnp.sum(jnp.where(bits, power, 0.0), axis=1, keepdims=True).astype(jnp.int32)

    mask = half(valid & (lane < 16)) + (half(valid & (lane >= 16)) << 16)
    plan_ref[...] = jnp.where(lane == 48, mask, jnp.where(valid, position, table))


def encode(target, row, slot, source):
    return (((target << 7) + row << 5) + slot << 6) + source


def list_near(table_ref, list_ref):
    def visit(i, count):
        row, slot = i >> 5, i & 31
        entry = table_ref[row, slot]
        list_ref[count] = encode(row, row, slot, entry & 63)
        return count + ((entry >= 0) & (entry < 8)).astype(jnp.int32)

    return pad_list(list_ref, lax.fori_loop(0, 8 * 32, visit, jnp.int32(0), unroll=8))


def list_far(targets, rows_ref, first, plan_ref, list_ref):
    def append(state, target, row):
        bits, count = state
        slot = 31 - lax.clz(bits & -bits)
        list_ref[count] = encode(target, row, slot, plan_ref[row, slot])
        return bits & (bits - 1), count + 1

    def visit(target, count):
        row = rows_ref[first + target]
        add = functools.partial(append, target=target, row=row)
        return lax.while_loop(lambda s: s[0] != 0, add, (plan_ref[row, 48], count))[1]

    return pad_list(list_ref, lax.fori_loop(0, targets, visit, jnp.int32(0)))


def pad_list(list_ref, count):
    for j in range(UNROLL):
        list_ref[count + j] = 0
    return count


def add_terms(count, list_ref, plan_ref, coef_ref, source_ref, left_ref, right_ref, out_ref):
    modes = coef_ref.shape[0] // 2

    def step(i, carry):
        for j in range(UNROLL):
            t = i * UNROLL + j
            code = list_ref[t]
            slot = (code >> 6) & 31
            row = (code >> 11) & 127
            target = code >> 18
            k = slot & (modes - 1)
            weight = plan_ref[row, 2 * modes + k].astype(F32)
            down = slot >= modes
            live = t < count
            alpha = jnp.where(live, jnp.where(down, weight * coef_ref[k], 1.0), 0.0)
            beta = jnp.where(live & down, weight * coef_ref[modes + k], 0.0)
            a_re, a_im, b_re, b_im = products(left_ref[k], right_ref[k], source_ref[code & 63])
            out_ref[target, 0] += alpha * (a_im - b_im) + beta * (a_re + b_re)
            out_ref[target, 1] += beta * (a_im + b_im) - alpha * (a_re - b_re)
        return carry

    lax.fori_loop(0, (count + UNROLL - 1) // UNROLL, step, 0)


def own_kernel(
    table_ref, coef_ref, rate_ref, source_ref, q_ref, h_ref, out_ref, left_ref, right_ref, hl_ref, hr_ref, list_ref
):
    load_modes(q_ref, left_ref, right_ref)
    load_modes(h_ref, hl_ref, hr_ref)
    modes = q_ref.shape[0]

    def one(m, carry):
        u = source_ref[m]
        damp = jnp.float32(0)
        for k in range(modes):
            damp += table_ref[m, 2 * modes + k].astype(F32) * rate_ref[k]
        ra, ia, rb, ib = products(hl_ref[0], hr_ref[0], u)
        rc, ic, rd, im = products(hl_ref[1], hr_ref[1], u)
        comm_re = (ra - ic) - (rb - im)
        comm_im = (ia + rc) - (ib + rd)
        out_ref[m, 0] = comm_im - damp * u[0]
        out_ref[m, 1] = -comm_re - damp * u[1]
        return carry

    lax.fori_loop(0, source_ref.shape[0], one, 0)
    count = list_near(table_ref, list_ref)
    add_terms(count, list_ref, table_ref, coef_ref, source_ref, left_ref, right_ref, out_ref)


def far_kernel(pieces, plan_ref, coef_ref, rows_ref, q_ref, *refs):
    blocks, refs = refs[:pieces], refs[pieces:]
    outs, (source_ref, left_ref, right_ref, *lists, sems) = refs[:2], refs[2:]
    copies = []
    for part, (lo, hi, _) in enumerate(PARTS):
        size = hi - lo
        copies.append((blocks[0].at[pl.ds(lo, size)], source_ref.at[pl.ds(8 * lo, size)]))
        for stage in range(3):
            block = blocks[1 + 3 * part + stage]
            for b in range(1 << stage):
                src = block.at[pl.ds(b * (block.shape[0] >> stage), size)]
                copies.append((src, source_ref.at[pl.ds(8 * lo + (size << stage) + b * size, size)]))
    copies = [pltpu.make_async_copy(a, b, sems.at[i]) for i, (a, b) in enumerate(copies)]
    for copy in copies:
        copy.start()
    load_modes(q_ref, left_ref, right_ref)
    targets = outs[0].shape[0]

    def clear(m, carry):
        for out in outs:
            out[m] = jnp.zeros(out.shape[1:], F32)
        return carry

    lax.fori_loop(0, targets, clear, 0)
    counts = [list_far(targets, rows_ref, i * targets, plan_ref, lists[i]) for i in range(2)]
    for copy in copies:
        copy.wait()
    for out, terms, count in zip(outs, lists, counts):
        add_terms(count, terms, plan_ref, coef_ref, source_ref, left_ref, right_ref, out)


def spec(space):
    return pl.BlockSpec(memory_space=space)


def params(mib):
    return pltpu.CompilerParams(vmem_limit_bytes=mib << 20)


def mode_scratch(modes, n):
    return [pltpu.VMEM((modes, 2 * n, 2 * n), BF16)] * 2


def cost(terms, n):
    return pl.CostEstimate(flops=terms * 4 * (2 * n) ** 3, bytes_accessed=1 << 23, transcendentals=0)


def served_rows(rc):
    rows = []
    for high in (1, 0):
        for lo, hi, order in PARTS:
            weight = ["xyz".index(a) for a in order]
            for second, third in np.ndindex(2, 2):
                b = 2 * ((high << weight[0]) + (second << weight[1]) + (third << weight[2])) + rc
                rows += [b * 8 + m for m in range(lo, hi)]
    return np.array(rows, np.int32)


def body(
    state,
    hamiltonian,
    couplings,
    bath_coef,
    bath_rate,
    occupation,
    send_list,
    up_index,
    down_index,
    step,
):
    local, _, n, _ = state.shape
    modes = couplings.shape[0]
    devices = send_list.shape[1]
    bit = {a: lax.axis_index(a) for a in ALL}
    at = jnp.stack([2 * bit[a + "h"] + bit[a + "l"] for a in "xyz"] + [bit["c"]]).astype(jnp.int32)
    pairs = {a: cell_pairs(a) for a in "xyz"}

    held = [[state[lo:hi]] for lo, hi, _ in PARTS]
    note = jnp.zeros((1, 2, n, n), F32).at[0, 0, 0, :devices].set(send_list.reshape(devices).astype(F32))
    held[2][0] = jnp.concatenate([held[2][0], note], axis=0)
    table = jnp.concatenate(
        [up_index, down_index, occupation, jnp.zeros((local, devices - 3 * modes), jnp.int32)], axis=1
    )
    tables = jnp.concatenate([table, flip(table, "c")], axis=0)
    for stage in range(3):
        sends = [part[0] if stage == 0 else jnp.concatenate(part, axis=0) for part in held]
        sends, tables = lax.optimization_barrier((sends, tables))
        for part, block, (_, _, order) in zip(held, sends, PARTS):
            part.append(lax.ppermute(block, ALL, pairs[order[stage]]))
        other = flip(tables, "xyz"[stage] + "h")
        if stage < 2:
            tables = jnp.concatenate([tables, other], axis=0)
    lists = jnp.concatenate([block[2::3, 0, 0, :devices] for block in held[2]], axis=0)

    smem, vmem = spec(pltpu.SMEM), spec(pltpu.VMEM)
    plan = pl.pallas_call(
        plan_kernel,
        out_shape=jax.ShapeDtypeStruct((2 * tables.shape[0], devices), jnp.int32),
        in_specs=[smem] + [vmem] * 3,
        out_specs=vmem,
    )(at, tables, other, lists)

    coef = bath_coef.reshape(-1)
    here, _ = lax.optimization_barrier((state, sends))
    listing = pltpu.SMEM((1024 + UNROLL,), jnp.int32)
    own = pl.pallas_call(
        own_kernel,
        out_shape=jax.ShapeDtypeStruct(state.shape, F32),
        in_specs=[smem] * 3 + [vmem] * 3,
        out_specs=vmem,
        scratch_shapes=mode_scratch(modes, n) + mode_scratch(2, n) + [listing],
        compiler_params=params(16),
        cost_estimate=cost(160, n),
    )(table, coef, bath_rate, here, couplings, hamiltonian)

    blocks = [state] + [block for part in held for block in part[1:]]
    own, plan = lax.optimization_barrier((own, plan))
    target = jax.ShapeDtypeStruct((4 * local, 2, n, n), F32)
    partial = []
    for rc in (1, 0):
        partial += pl.pallas_call(
            functools.partial(far_kernel, len(blocks)),
            out_shape=(target, target),
            in_specs=[smem] * 3 + [vmem] + [spec(pl.ANY)] * len(blocks),
            out_specs=(vmem, vmem),
            scratch_shapes=[pltpu.VMEM((8 * local, 2, n, n), F32)]
            + mode_scratch(modes, n)
            + [listing, listing, pltpu.SemaphoreType.DMA((24,))],
            compiler_params=params(28),
            cost_estimate=cost(48, n),
        )(plan, coef, served_rows(rc), couplings, *blocks)
    swapped = [flip(partial[0], "c"), flip(partial[1], "c")]
    sums = []
    for lo, hi, axes in PARTS:
        rows = slice(4 * lo, 4 * hi)
        give = partial[2][rows] + swapped[0][rows]
        keep = partial[3][rows] + swapped[1][rows]
        for stage in range(3):
            keep = keep + flip(give, axes[stage] + "h")
            half = keep.shape[0] // 2
            if stage < 2:
                keep, give = keep[:half], keep[half:]
        sums.append(keep)
    derivative = own + jnp.concatenate(sums, axis=0)

    total = jnp.sum(derivative * derivative)
    total = jnp.sum(
        lax.all_to_all(jnp.broadcast_to(total, (devices,)), ALL, split_axis=0, concat_axis=0, tiled=True)
    )
    rms = jnp.sqrt(total / (devices * derivative.size) + 1e-06)
    return derivative, state + step[0] / rms * derivative


def solution(mesh):
    torus = Mesh(mesh.devices.reshape((2,) * 7), ALL)
    whole = P(ALL, None, None, None)
    index = P(ALL, None)
    in_specs = (whole, P(), P(), P(), P(), index, P(ALL, None, None), index, index, P())
    return jax.shard_map(body, mesh=torus, in_specs=in_specs, out_specs=(whole, whole), check_vma=False)
```

```python
import functools

import jax
import jax.numpy as jnp
import numpy as np
from jax import lax
from jax.experimental import pallas as pl
from jax.experimental.pallas import tpu as pltpu
from jax.sharding import Mesh
from jax.sharding import PartitionSpec as P

ALL = ("xh", "xl", "c", "yh", "yl", "zh", "zl")
UNROLL = 4
F32 = jnp.float32
BF16 = jnp.bfloat16
PARTS = ((0, 3, "xyz"), (3, 6, "yzx"), (6, 8, "zxy"))


def dot(a, b):
    return jnp.dot(a, b, preferred_element_type=F32)


def cell_pairs(axis):
    pairs = []
    for x, c, y, z in np.ndindex(4, 2, 4, 4):
        at = {"x": x, "y": y, "z": z}
        to = dict(at)
        to[axis] = (((at[axis] + c) % 4 ^ 1) - c) % 4
        pairs.append((((x * 2 + c) * 4 + y) * 4 + z, ((to["x"] * 2 + c) * 4 + to["y"]) * 4 + to["z"]))
    return pairs


def flip(value, axis):
    return lax.ppermute(value, axis, [(0, 1), (1, 0)])


def split(value):
    high = value.astype(BF16)
    return high, (value - high.astype(F32)).astype(BF16)


def load_modes(q_ref, left_ref, right_ref):
    n = q_ref.shape[-1]

    def one(k, carry):
        high, low = split(q_ref[k])
        left_ref[k, :n, :n] = high
        left_ref[k, :n, n:] = high
        left_ref[k, n:, :n] = low
        left_ref[k, n:, n:] = low
        right_ref[k, :n, :n] = high
        right_ref[k, :n, n:] = low
        right_ref[k, n:, :n] = high
        right_ref[k, n:, n:] = low
        return carry

    lax.fori_loop(0, q_ref.shape[0], one, 0)


def products(left, right, u):
    n = u.shape[-1]
    high, low = split(u)
    tall = jnp.concatenate(
        [jnp.concatenate([high[0], high[1]], axis=1), jnp.concatenate([low[0], low[1]], axis=1)], axis=0
    )
    z = dot(left, tall)
    z = z[:n] + z[n:]
    wide = jnp.concatenate([high.reshape(2 * n, n), low.reshape(2 * n, n)], axis=1)
    w = dot(wide, right)
    w = w[:, :n] + w[:, n:]
    return z[:, :n], z[:, n:], w[:n], w[n:]


def plan_kernel(at_ref, low_ref, high_ref, lists_ref, plan_ref):
    x, y, z, c = (at_ref[i] for i in range(4))
    table = jnp.concatenate([low_ref[...], high_ref[...]], axis=0)
    row = lax.broadcasted_iota(jnp.int32, table.shape, 0) >> 3
    lane = lax.broadcasted_iota(jnp.int32, table.shape, 1)
    dx, dy, dz = x ^ (row & 2), y ^ ((row & 4) >> 1), z ^ ((row & 8) >> 2)
    device = (((dx << 1) + (c ^ (row & 1)) << 2) + dy << 2) + dz
    chosen = jnp.where(lane == device, 1.0, 0.0)
    listed = lax.dot_general(
        chosen, lists_ref[...], (((1,), (1,)), ((), ())), preferred_element_type=F32
    )
    far = table - 8
    owner = {"x": far >> 5, "y": (far >> 2) & 3, "z": far & 3}
    inside = (far >= 0) & (((far >> 4) & 1) == c) & (lane < 32)
    differs = {}
    for a, ours in zip("xyz", (x, y, z)):
        theirs, ours = (owner[a] + c) & 3, (ours + c) & 3
        inside = inside & ((theirs >> 1) == (ours >> 1))
        differs[a] = (theirs ^ ours) & 1
    member = sum(differs[a] << s for s, a in enumerate(PARTS[2][2]))
    slot = jnp.full(table.shape, -1.0, F32)
    for b in range(8):
        slot = jnp.where(member == b, listed[:, b : b + 1], slot)
    slot = slot.astype(jnp.int32)
    position = jnp.zeros(table.shape, jnp.int32)
    for lo, hi, order in PARTS:
        block = sum(differs[a] << s for s, a in enumerate(order))
        position = jnp.where((slot >= lo) & (slot < hi), 8 * lo + block * (hi - lo) + slot - lo, position)
    valid = inside & (slot >= 0)
    power = (1 << (lane & 15)).astype(F32)

    def half(bits):
        return jnp.sum(jnp.where(bits, power, 0.0), axis=1, keepdims=True).astype(jnp.int32)

    mask = half(valid & (lane < 16)) + (half(valid & (lane >= 16)) << 16)
    plan_ref[...] = jnp.where(lane == 48, mask, jnp.where(valid, position, table))


def encode(target, row, slot, source):
    return (((target << 7) + row << 5) + slot << 6) + source


def list_near(table_ref, list_ref):
    def visit(i, count):
        row, slot = i >> 5, i & 31
        entry = table_ref[row, slot]
        list_ref[count] = encode(row, row, slot, entry & 63)
        return count + ((entry >= 0) & (entry < 8)).astype(jnp.int32)

    return pad_list(list_ref, lax.fori_loop(0, 8 * 32, visit, jnp.int32(0), unroll=8))


def list_far(targets, rows_ref, first, plan_ref, list_ref):
    def append(state, target, row):
        bits, count = state
        slot = 31 - lax.clz(bits & -bits)
        list_ref[count] = encode(target, row, slot, plan_ref[row, slot])
        return bits & (bits - 1), count + 1

    def visit(target, count):
        row = rows_ref[first + target]
        add = functools.partial(append, target=target, row=row)
        return lax.while_loop(lambda s: s[0] != 0, add, (plan_ref[row, 48], count))[1]

    return pad_list(list_ref, lax.fori_loop(0, targets, visit, jnp.int32(0)))


def pad_list(list_ref, count):
    for j in range(UNROLL):
        list_ref[count + j] = 0
    return count


def add_terms(count, list_ref, plan_ref, coef_ref, source_ref, left_ref, right_ref, out_ref):
    modes = coef_ref.shape[0] // 2

    def step(i, carry):
        for j in range(UNROLL):
            t = i * UNROLL + j
            code = list_ref[t]
            slot = (code >> 6) & 31
            row = (code >> 11) & 127
            target = code >> 18
            k = slot & (modes - 1)
            weight = plan_ref[row, 2 * modes + k].astype(F32)
            down = slot >= modes
            live = t < count
            alpha = jnp.where(live, jnp.where(down, weight * coef_ref[k], 1.0), 0.0)
            beta = jnp.where(live & down, weight * coef_ref[modes + k], 0.0)
            a_re, a_im, b_re, b_im = products(left_ref[k], right_ref[k], source_ref[code & 63])
            out_ref[target, 0] += alpha * (a_im - b_im) + beta * (a_re + b_re)
            out_ref[target, 1] += beta * (a_im + b_im) - alpha * (a_re - b_re)
        return carry

    lax.fori_loop(0, (count + UNROLL - 1) // UNROLL, step, 0)


def own_kernel(
    table_ref, coef_ref, rate_ref, source_ref, left_ref, right_ref, h_ref, out_ref, hl_ref, hr_ref, list_ref
):
    load_modes(h_ref, hl_ref, hr_ref)
    modes = left_ref.shape[0]

    def one(m, carry):
        u = source_ref[m]
        damp = jnp.float32(0)
        for k in range(modes):
            damp += table_ref[m, 2 * modes + k].astype(F32) * rate_ref[k]
        ra, ia, rb, ib = products(hl_ref[0], hr_ref[0], u)
        rc, ic, rd, im = products(hl_ref[1], hr_ref[1], u)
        comm_re = (ra - ic) - (rb - im)
        comm_im = (ia + rc) - (ib + rd)
        out_ref[m, 0] = comm_im - damp * u[0]
        out_ref[m, 1] = -comm_re - damp * u[1]
        return carry

    lax.fori_loop(0, source_ref.shape[0], one, 0)
    count = list_near(table_ref, list_ref)
    add_terms(count, list_ref, table_ref, coef_ref, source_ref, left_ref, right_ref, out_ref)


HELD = ((0, 1), (1, 1), (2, 2), (4, 4))


def clear(out_ref):
    def one(m, carry):
        out_ref[m] = jnp.zeros(out_ref.shape[1:], F32)
        return carry

    lax.fori_loop(0, out_ref.shape[0], one, 0)


def block_copies(blocks, stages, source_ref, sems):
    copies = []
    for (lo, hi, _), part in zip(PARTS, blocks):
        size = hi - lo
        for block, (first, members) in zip(part, (HELD[i] for i in stages)):
            for b in range(members):
                src = block.at[pl.ds(b * (block.shape[0] // members), size)]
                copies.append((src, source_ref.at[pl.ds(8 * lo + (first + b) * size, size)]))
    return [pltpu.make_async_copy(a, b, sems.at[i]) for i, (a, b) in enumerate(copies)]


def early_kernel(q_ref, *refs):
    blocks, (source_ref, left_ref, right_ref, sems) = refs[:-4], refs[-4:]
    own = [blocks[0].at[pl.ds(lo, hi - lo)] for lo, hi, _ in PARTS]
    parts = [[own[i], *blocks[1 + 2 * i : 3 + 2 * i]] for i in range(len(PARTS))]
    copies = block_copies(parts, (0, 1, 2), source_ref, sems)
    for copy in copies:
        copy.start()
    load_modes(q_ref, left_ref, right_ref)
    for copy in copies:
        copy.wait()


def first_kernel(
    plan_ref, coef_ref, rows_ref, left_ref, right_ref, _, a_ref, b_ref, c_ref, source_ref, out_ref, list_ref, sems
):
    copies = block_copies([[a_ref], [b_ref], [c_ref]], (3,), source_ref, sems)
    for copy in copies:
        copy.start()
    count = list_far(out_ref.shape[0], rows_ref, 0, plan_ref, list_ref)
    clear(out_ref)
    for copy in copies:
        copy.wait()
    add_terms(count, list_ref, plan_ref, coef_ref, source_ref, left_ref, right_ref, out_ref)


def next_kernel(outs, plan_ref, coef_ref, rows_ref, source_ref, left_ref, right_ref, *refs):
    list_ref = refs[outs]
    for i, out_ref in enumerate(refs[:outs]):
        targets = out_ref.shape[0]
        count = list_far(targets, rows_ref, i * targets, plan_ref, list_ref)
        clear(out_ref)
        add_terms(count, list_ref, plan_ref, coef_ref, source_ref, left_ref, right_ref, out_ref)


def spec(space):
    return pl.BlockSpec(memory_space=space)


def params(mib):
    return pltpu.CompilerParams(vmem_limit_bytes=mib << 20)


def mode_scratch(modes, n):
    return [pltpu.VMEM((modes, 2 * n, 2 * n), BF16)] * 2


def cost(terms, n):
    return pl.CostEstimate(flops=terms * 4 * (2 * n) ** 3, bytes_accessed=1 << 23, transcendentals=0)


def served_rows(rc, high):
    rows = []
    for lo, hi, order in PARTS:
        weight = ["xyz".index(a) for a in order]
        for second, third in np.ndindex(2, 2):
            b = 2 * ((high << weight[0]) + (second << weight[1]) + (third << weight[2])) + rc
            rows += [b * 8 + m for m in range(lo, hi)]
    return np.array(rows, np.int32)


def body(
    state,
    hamiltonian,
    couplings,
    bath_coef,
    bath_rate,
    occupation,
    send_list,
    up_index,
    down_index,
    step,
):
    local, _, n, _ = state.shape
    modes = couplings.shape[0]
    devices = send_list.shape[1]
    bit = {a: lax.axis_index(a) for a in ALL}
    at = jnp.stack([2 * bit[a + "h"] + bit[a + "l"] for a in "xyz"] + [bit["c"]]).astype(jnp.int32)
    pairs = {a: cell_pairs(a) for a in "xyz"}

    held = [[state[lo:hi]] for lo, hi, _ in PARTS]
    note = jnp.zeros((1, 2, n, n), F32).at[0, 0, 0, :devices].set(send_list.reshape(devices).astype(F32))
    held[2][0] = jnp.concatenate([held[2][0], note], axis=0)
    table = jnp.concatenate(
        [up_index, down_index, occupation, jnp.zeros((local, devices - 3 * modes), jnp.int32)], axis=1
    )
    tables = jnp.concatenate([table, flip(table, "c")], axis=0)
    for stage in range(3):
        sends = [part[0] if stage == 0 else jnp.concatenate(part, axis=0) for part in held]
        sends, tables = lax.optimization_barrier((sends, tables))
        for part, block, (_, _, order) in zip(held, sends, PARTS):
            part.append(lax.ppermute(block, ALL, pairs[order[stage]]))
        other = flip(tables, "xyz"[stage] + "h")
        if stage < 2:
            tables = jnp.concatenate([tables, other], axis=0)
    lists = jnp.concatenate([block[2::3, 0, 0, :devices] for block in held[2]], axis=0)

    smem, vmem = spec(pltpu.SMEM), spec(pltpu.VMEM)
    plan = pl.pallas_call(
        plan_kernel,
        out_shape=jax.ShapeDtypeStruct((2 * tables.shape[0], devices), jnp.int32),
        in_specs=[smem] + [vmem] * 3,
        out_specs=vmem,
        compiler_params=params(4),
    )(at, tables, other, lists)

    coef = bath_coef.reshape(-1)
    listing = pltpu.SMEM((1024 + UNROLL,), jnp.int32)
    target = jax.ShapeDtypeStruct((4 * local, 2, n, n), F32)
    half_modes = jax.ShapeDtypeStruct((modes, 2 * n, 2 * n), BF16)

    everything = jax.ShapeDtypeStruct((8 * local, 2, n, n), F32)
    early, late = [state], []
    for part in held:
        early += part[1:3]
        late.append(part[3])
    early, _ = lax.optimization_barrier((early, sends))
    early, late = ([pltpu.with_memory_space_constraint(b, pltpu.HBM) for b in group] for group in (early, late))
    source, left, right = pl.pallas_call(
        early_kernel,
        out_shape=(everything, half_modes, half_modes),
        in_specs=[vmem] + [spec(pltpu.HBM)] * len(early),
        out_specs=(vmem,) * 3,
        scratch_shapes=[pltpu.SemaphoreType.DMA((12,))],
        compiler_params=params(20),
        cost_estimate=cost(160, n),
    )(couplings, *early)

    source, other = pl.pallas_call(
        first_kernel,
        out_shape=(everything, target),
        in_specs=[smem] * 3 + [vmem] * 3 + [spec(pltpu.HBM)] * 3,
        out_specs=(vmem,) * 2,
        scratch_shapes=[listing, pltpu.SemaphoreType.DMA((12,))],
        input_output_aliases={5: 0},
        compiler_params=params(24),
        cost_estimate=cost(32, n),
    )(plan, coef, served_rows(1, 1), left, right, source, *late)
    parts = [slice(4 * lo, 4 * hi) for lo, hi, _ in PARTS]
    swapped = flip(other, "c")

    def later(plan, rows, outs):
        return pl.pallas_call(
            functools.partial(next_kernel, outs),
            out_shape=(target,) * outs,
            in_specs=[smem] * 3 + [vmem] * 3,
            out_specs=(vmem,) * outs,
            scratch_shapes=[listing],
            compiler_params=params(24),
            cost_estimate=cost(24 * outs, n),
        )(plan, coef, rows, source, left, right)

    same, other = later(plan, np.concatenate([served_rows(0, 1), served_rows(1, 0)]), 2)
    gives = [same[rows] + swapped[rows] for rows in parts]

    here, plan, gives, other = lax.optimization_barrier((state, plan, gives, other))
    swapped = flip(other, "c")
    own = pl.pallas_call(
        own_kernel,
        out_shape=jax.ShapeDtypeStruct(state.shape, F32),
        in_specs=[smem] * 3 + [vmem] * 4,
        out_specs=vmem,
        scratch_shapes=mode_scratch(2, n) + [listing],
        compiler_params=params(16),
        cost_estimate=cost(160, n),
    )(table, coef, bath_rate, here, left, right, hamiltonian)
    (kept,) = later(plan, served_rows(0, 0), 1)
    keeps = [kept[rows] + swapped[rows] for rows in parts]
    keeps, own = lax.optimization_barrier((keeps, own))

    sums = []
    for give, keep, (_, _, axes) in zip(gives, keeps, PARTS):
        for stage in range(3):
            keep = keep + flip(give, axes[stage] + "h")
            half = keep.shape[0] // 2
            if stage < 2:
                keep, give = keep[:half], keep[half:]
        sums.append(keep)
    derivative = own + jnp.concatenate(sums, axis=0)

    total = jnp.sum(derivative * derivative)
    total = jnp.sum(
        lax.all_to_all(jnp.broadcast_to(total, (devices,)), ALL, split_axis=0, concat_axis=0, tiled=True)
    )
    rms = jnp.sqrt(total / (devices * derivative.size) + 1e-06)
    return derivative, state + step[0] / rms * derivative


def solution(mesh):
    torus = Mesh(mesh.devices.reshape((2,) * 7), ALL)
    whole = P(ALL, None, None, None)
    index = P(ALL, None)
    in_specs = (whole, P(), P(), P(), P(), index, P(ALL, None, None), index, index, P())
    return jax.shard_map(body, mesh=torus, in_specs=in_specs, out_specs=(whole, whole), check_vma=False)
```

```python
import functools

import jax
import jax.numpy as jnp
import numpy as np
from jax import lax
from jax.experimental import pallas as pl
from jax.experimental.pallas import tpu as pltpu
from jax.sharding import Mesh
from jax.sharding import PartitionSpec as P

ALL = ("xh", "xl", "c", "yh", "yl", "zh", "zl")
UNROLL = 4
F32 = jnp.float32
BF16 = jnp.bfloat16
PARTS = ((0, 3, "xyz"), (3, 6, "yzx"), (6, 8, "zxy"))


def dot(a, b):
    return jnp.dot(a, b, preferred_element_type=F32)


def cell_pairs(axis):
    pairs = []
    for x, c, y, z in np.ndindex(4, 2, 4, 4):
        at = {"x": x, "y": y, "z": z}
        to = dict(at)
        to[axis] = (((at[axis] + c) % 4 ^ 1) - c) % 4
        pairs.append((((x * 2 + c) * 4 + y) * 4 + z, ((to["x"] * 2 + c) * 4 + to["y"]) * 4 + to["z"]))
    return pairs


def flip(value, axis):
    return lax.ppermute(value, axis, [(0, 1), (1, 0)])


def split(value):
    high = value.astype(BF16)
    return high, (value - high.astype(F32)).astype(BF16)


def load_modes(q_ref, left_ref, right_ref):
    n = q_ref.shape[-1]

    def one(k, carry):
        high, low = split(q_ref[k])
        left_ref[k, :n, :n] = high
        left_ref[k, :n, n:] = high
        left_ref[k, n:, :n] = low
        left_ref[k, n:, n:] = low
        right_ref[k, :n, :n] = high
        right_ref[k, :n, n:] = low
        right_ref[k, n:, :n] = high
        right_ref[k, n:, n:] = low
        return carry

    lax.fori_loop(0, q_ref.shape[0], one, 0)


def products(left, right, u):
    n = u.shape[-1]
    high, low = split(u)
    tall = jnp.concatenate(
        [jnp.concatenate([high[0], high[1]], axis=1), jnp.concatenate([low[0], low[1]], axis=1)], axis=0
    )
    z = dot(left, tall)
    z = z[:n] + z[n:]
    wide = jnp.concatenate([high.reshape(2 * n, n), low.reshape(2 * n, n)], axis=1)
    w = dot(wide, right)
    w = w[:, :n] + w[:, n:]
    return z[:, :n], z[:, n:], w[:n], w[n:]


def plan_kernel(at_ref, low_ref, high_ref, lists_ref, plan_ref):
    x, y, z, c = (at_ref[i] for i in range(4))
    table = jnp.concatenate([low_ref[...], high_ref[...]], axis=0)
    row = lax.broadcasted_iota(jnp.int32, table.shape, 0) >> 3
    lane = lax.broadcasted_iota(jnp.int32, table.shape, 1)
    dx, dy, dz = x ^ (row & 2), y ^ ((row & 4) >> 1), z ^ ((row & 8) >> 2)
    device = (((dx << 1) + (c ^ (row & 1)) << 2) + dy << 2) + dz
    chosen = jnp.where(lane == device, 1.0, 0.0)
    listed = lax.dot_general(
        chosen, lists_ref[...], (((1,), (1,)), ((), ())), preferred_element_type=F32
    )
    far = table - 8
    owner = {"x": far >> 5, "y": (far >> 2) & 3, "z": far & 3}
    inside = (far >= 0) & (((far >> 4) & 1) == c) & (lane < 32)
    differs = {}
    for a, ours in zip("xyz", (x, y, z)):
        theirs, ours = (owner[a] + c) & 3, (ours + c) & 3
        inside = inside & ((theirs >> 1) == (ours >> 1))
        differs[a] = (theirs ^ ours) & 1
    member = sum(differs[a] << s for s, a in enumerate(PARTS[2][2]))
    slot = jnp.full(table.shape, -1.0, F32)
    for b in range(8):
        slot = jnp.where(member == b, listed[:, b : b + 1], slot)
    slot = slot.astype(jnp.int32)
    position = jnp.zeros(table.shape, jnp.int32)
    for lo, hi, order in PARTS:
        block = sum(differs[a] << s for s, a in enumerate(order))
        place = 8 * lo + block * (hi - lo) + slot - lo + ((block >> 2) << 6)
        position = jnp.where((slot >= lo) & (slot < hi), place, position)
    valid = inside & (slot >= 0)
    power = (1 << (lane & 15)).astype(F32)

    def half(bits):
        return jnp.sum(jnp.where(bits, power, 0.0), axis=1, keepdims=True).astype(jnp.int32)

    mask = half(valid & (lane < 16)) + (half(valid & (lane >= 16)) << 16)
    plan_ref[...] = jnp.where(lane == 48, mask, jnp.where(valid, position, table))


def encode(target, row, slot, source):
    return (((target << 7) + row << 5) + slot << 6) + source


def list_near(table_ref, list_ref):
    def visit(i, count):
        row, slot = i >> 5, i & 31
        entry = table_ref[row, slot]
        list_ref[count] = encode(row, row, slot, entry & 63)
        return count + ((entry >= 0) & (entry < 8)).astype(jnp.int32)

    return pad_list(list_ref, lax.fori_loop(0, 8 * 32, visit, jnp.int32(0), unroll=8))


def list_far(targets, rows_ref, first, plan_ref, list_ref):
    def append(state, target, row):
        bits, count = state
        slot = 31 - lax.clz(bits & -bits)
        list_ref[count] = encode(target, row, slot, plan_ref[row, slot] & 63)
        return bits & (bits - 1), count + 1

    def visit(target, count):
        row = rows_ref[first + target]
        add = functools.partial(append, target=target, row=row)
        return lax.while_loop(lambda s: s[0] != 0, add, (plan_ref[row, 48], count))[1]

    return pad_list(list_ref, lax.fori_loop(0, targets, visit, jnp.int32(0)))


def list_split(targets, rows_ref, plan_ref, early_ref, late_ref):
    def append(state, target, row):
        bits, early, late = state
        slot = 31 - lax.clz(bits & -bits)
        value = plan_ref[row, slot]
        code = encode(target, row, slot, value & 63)
        early_ref[early] = code
        late_ref[late] = code
        return bits & (bits - 1), early + 1 - (value >> 6), late + (value >> 6)

    def visit(target, counts):
        row = rows_ref[target]
        add = functools.partial(append, target=target, row=row)
        return lax.while_loop(lambda s: s[0] != 0, add, (plan_ref[row, 48], *counts))[1:]

    early, late = lax.fori_loop(0, targets, visit, (jnp.int32(0), jnp.int32(0)))
    return pad_list(early_ref, early), pad_list(late_ref, late)


def pad_list(list_ref, count):
    for j in range(UNROLL):
        list_ref[count + j] = 0
    return count


def add_terms(count, list_ref, plan_ref, coef_ref, source_ref, left_ref, right_ref, out_ref):
    modes = coef_ref.shape[0] // 2

    def step(i, carry):
        for j in range(UNROLL):
            t = i * UNROLL + j
            code = list_ref[t]
            slot = (code >> 6) & 31
            row = (code >> 11) & 127
            target = code >> 18
            k = slot & (modes - 1)
            weight = plan_ref[row, 2 * modes + k].astype(F32)
            down = slot >= modes
            live = t < count
            alpha = jnp.where(live, jnp.where(down, weight * coef_ref[k], 1.0), 0.0)
            beta = jnp.where(live & down, weight * coef_ref[modes + k], 0.0)
            a_re, a_im, b_re, b_im = products(left_ref[k], right_ref[k], source_ref[code & 63])
            out_ref[target, 0] += alpha * (a_im - b_im) + beta * (a_re + b_re)
            out_ref[target, 1] += beta * (a_im + b_im) - alpha * (a_re - b_re)
        return carry

    lax.fori_loop(0, (count + UNROLL - 1) // UNROLL, step, 0)


def own_kernel(
    table_ref, coef_ref, rate_ref, source_ref, left_ref, right_ref, h_ref, out_ref, hl_ref, hr_ref, list_ref
):
    load_modes(h_ref, hl_ref, hr_ref)
    modes = left_ref.shape[0]

    def one(m, carry):
        u = source_ref[m]
        damp = jnp.float32(0)
        for k in range(modes):
            damp += table_ref[m, 2 * modes + k].astype(F32) * rate_ref[k]
        ra, ia, rb, ib = products(hl_ref[0], hr_ref[0], u)
        rc, ic, rd, im = products(hl_ref[1], hr_ref[1], u)
        comm_re = (ra - ic) - (rb - im)
        comm_im = (ia + rc) - (ib + rd)
        out_ref[m, 0] = comm_im - damp * u[0]
        out_ref[m, 1] = -comm_re - damp * u[1]
        return carry

    lax.fori_loop(0, source_ref.shape[0], one, 0)
    count = list_near(table_ref, list_ref)
    add_terms(count, list_ref, table_ref, coef_ref, source_ref, left_ref, right_ref, out_ref)


HELD = ((0, 1), (1, 1), (2, 2), (4, 4))


def clear(out_ref):
    def one(m, carry):
        out_ref[m] = jnp.zeros(out_ref.shape[1:], F32)
        return carry

    lax.fori_loop(0, out_ref.shape[0], one, 0)


def block_copies(blocks, stages, source_ref, sems):
    copies = []
    for (lo, hi, _), part in zip(PARTS, blocks):
        size = hi - lo
        for block, (first, members) in zip(part, (HELD[i] for i in stages)):
            for b in range(members):
                src = block.at[pl.ds(b * (block.shape[0] // members), size)]
                copies.append((src, source_ref.at[pl.ds(8 * lo + (first + b) * size, size)]))
    return [pltpu.make_async_copy(a, b, sems.at[i]) for i, (a, b) in enumerate(copies)]


def early_kernel(q_ref, *refs):
    blocks, (source_ref, left_ref, right_ref, sems) = refs[:-4], refs[-4:]
    own = [blocks[0].at[pl.ds(lo, hi - lo)] for lo, hi, _ in PARTS]
    parts = [[own[i], *blocks[1 + 2 * i : 3 + 2 * i]] for i in range(len(PARTS))]
    copies = block_copies(parts, (0, 1, 2), source_ref, sems)
    for copy in copies:
        copy.start()
    load_modes(q_ref, left_ref, right_ref)
    for copy in copies:
        copy.wait()


def first_kernel(
    plan_ref, coef_ref, rows_ref, left_ref, right_ref, _, a_ref, b_ref, c_ref, source_ref, out_ref, *refs
):
    early_ref, late_ref, sems = refs
    copies = block_copies([[a_ref], [b_ref], [c_ref]], (3,), source_ref, sems)
    for copy in copies:
        copy.start()
    early, late = list_split(out_ref.shape[0], rows_ref, plan_ref, early_ref, late_ref)
    clear(out_ref)
    add_terms(early, early_ref, plan_ref, coef_ref, source_ref, left_ref, right_ref, out_ref)
    for copy in copies:
        copy.wait()
    add_terms(late, late_ref, plan_ref, coef_ref, source_ref, left_ref, right_ref, out_ref)


def next_kernel(outs, plan_ref, coef_ref, rows_ref, source_ref, left_ref, right_ref, *refs):
    list_ref = refs[outs]
    for i, out_ref in enumerate(refs[:outs]):
        targets = out_ref.shape[0]
        count = list_far(targets, rows_ref, i * targets, plan_ref, list_ref)
        clear(out_ref)
        add_terms(count, list_ref, plan_ref, coef_ref, source_ref, left_ref, right_ref, out_ref)


def derivative_kernel(own_ref, *refs):
    ins, (out_ref, again_ref, total_ref) = refs[:-3], refs[-3:]
    squares = jnp.zeros(own_ref.shape[2:], F32)
    for i, (lo, hi, _) in enumerate(PARTS):
        keep_ref, mate_ref = ins[2 * i : 2 * i + 2]
        for m in range(lo, hi):
            for part in range(2):
                value = own_ref[m, part] + (keep_ref[m - lo, part] + mate_ref[m - lo, part])
                out_ref[m, part] = value
                again_ref[m, part] = value
                squares += value * value
    total = jnp.sum(jnp.sum(squares, axis=0, keepdims=True), axis=1, keepdims=True)
    total_ref[...] = jnp.broadcast_to(total.reshape(1, 1, 1), total_ref.shape)


def advance_kernel(step_ref, totals_ref, derivative_ref, state_ref, out_ref):
    total = jnp.sum(totals_ref[...], axis=0)
    rms = jnp.sqrt(total / (totals_ref.shape[0] * derivative_ref.size) + 1e-06)
    scale = step_ref[0] / rms
    for m in range(out_ref.shape[0]):
        for part in range(2):
            out_ref[m, part] = state_ref[m, part] + scale * derivative_ref[m, part]


def spec(space):
    return pl.BlockSpec(memory_space=space)


def params(mib):
    return pltpu.CompilerParams(vmem_limit_bytes=mib << 20)


def mode_scratch(modes, n):
    return [pltpu.VMEM((modes, 2 * n, 2 * n), BF16)] * 2


def cost(terms, n):
    return pl.CostEstimate(flops=terms * 4 * (2 * n) ** 3, bytes_accessed=1 << 23, transcendentals=0)


def served_rows(rc, high):
    rows = []
    for lo, hi, order in PARTS:
        weight = ["xyz".index(a) for a in order]
        for second, third in np.ndindex(2, 2):
            b = 2 * ((high << weight[0]) + (second << weight[1]) + (third << weight[2])) + rc
            rows += [b * 8 + m for m in range(lo, hi)]
    return np.array(rows, np.int32)


def body(
    state,
    hamiltonian,
    couplings,
    bath_coef,
    bath_rate,
    occupation,
    send_list,
    up_index,
    down_index,
    step,
):
    local, _, n, _ = state.shape
    modes = couplings.shape[0]
    devices = send_list.shape[1]
    bit = {a: lax.axis_index(a) for a in ALL}
    at = jnp.stack([2 * bit[a + "h"] + bit[a + "l"] for a in "xyz"] + [bit["c"]]).astype(jnp.int32)
    pairs = {a: cell_pairs(a) for a in "xyz"}

    held = [[state[lo:hi]] for lo, hi, _ in PARTS]
    note = jnp.zeros((1, 2, n, n), F32).at[0, 0, 0, :devices].set(send_list.reshape(devices).astype(F32))
    held[2][0] = jnp.concatenate([held[2][0], note], axis=0)
    table = jnp.concatenate(
        [up_index, down_index, occupation, jnp.zeros((local, devices - 3 * modes), jnp.int32)], axis=1
    )
    tables = jnp.concatenate([table, flip(table, "c")], axis=0)
    for stage in range(3):
        sends = [part[0] if stage == 0 else jnp.concatenate(part, axis=0) for part in held]
        sends, tables = lax.optimization_barrier((sends, tables))
        for part, block, (_, _, order) in zip(held, sends, PARTS):
            part.append(lax.ppermute(block, ALL, pairs[order[stage]]))
        other = flip(tables, "xyz"[stage] + "h")
        if stage < 2:
            tables = jnp.concatenate([tables, other], axis=0)
    lists = jnp.concatenate([block[2::3, 0, 0, :devices] for block in held[2]], axis=0)

    smem, vmem = spec(pltpu.SMEM), spec(pltpu.VMEM)
    plan = pl.pallas_call(
        plan_kernel,
        out_shape=jax.ShapeDtypeStruct((2 * tables.shape[0], devices), jnp.int32),
        in_specs=[smem] + [vmem] * 3,
        out_specs=vmem,
        compiler_params=params(4),
    )(at, tables, other, lists)

    coef = bath_coef.reshape(-1)
    listing = pltpu.SMEM((1024 + UNROLL,), jnp.int32)
    target = jax.ShapeDtypeStruct((4 * local, 2, n, n), F32)
    half_modes = jax.ShapeDtypeStruct((modes, 2 * n, 2 * n), BF16)

    everything = jax.ShapeDtypeStruct((8 * local, 2, n, n), F32)
    early, late = [state], []
    for part in held:
        early += part[1:3]
        late.append(part[3])
    early, _ = lax.optimization_barrier((early, sends))
    early, late = ([pltpu.with_memory_space_constraint(b, pltpu.HBM) for b in group] for group in (early, late))
    source, left, right = pl.pallas_call(
        early_kernel,
        out_shape=(everything, half_modes, half_modes),
        in_specs=[vmem] + [spec(pltpu.HBM)] * len(early),
        out_specs=(vmem,) * 3,
        scratch_shapes=[pltpu.SemaphoreType.DMA((12,))],
        compiler_params=params(20),
        cost_estimate=cost(160, n),
    )(couplings, *early)

    source, other = pl.pallas_call(
        first_kernel,
        out_shape=(everything, target),
        in_specs=[smem] * 3 + [vmem] * 3 + [spec(pltpu.HBM)] * 3,
        out_specs=(vmem,) * 2,
        scratch_shapes=[listing, listing, pltpu.SemaphoreType.DMA((12,))],
        input_output_aliases={5: 0},
        compiler_params=params(24),
        cost_estimate=cost(32, n),
    )(plan, coef, served_rows(1, 1), left, right, source, *late)
    parts = [slice(4 * lo, 4 * hi) for lo, hi, _ in PARTS]
    swapped = flip(other, "c")

    def later(plan, rows, outs):
        return pl.pallas_call(
            functools.partial(next_kernel, outs),
            out_shape=(target,) * outs,
            in_specs=[smem] * 3 + [vmem] * 3,
            out_specs=(vmem,) * outs,
            scratch_shapes=[listing],
            compiler_params=params(24),
            cost_estimate=cost(24 * outs, n),
        )(plan, coef, rows, source, left, right)

    same, other = later(plan, np.concatenate([served_rows(0, 1), served_rows(1, 0)]), 2)
    gives = [same[rows] + swapped[rows] for rows in parts]

    here, plan, gives, other = lax.optimization_barrier((state, plan, gives, other))
    swapped = flip(other, "c")
    own = pl.pallas_call(
        own_kernel,
        out_shape=jax.ShapeDtypeStruct(state.shape, F32),
        in_specs=[smem] * 3 + [vmem] * 4,
        out_specs=vmem,
        scratch_shapes=mode_scratch(2, n) + [listing],
        compiler_params=params(16),
        cost_estimate=cost(160, n),
    )(table, coef, bath_rate, here, left, right, hamiltonian)
    (kept,) = later(plan, served_rows(0, 0), 1)
    keeps = [kept[rows] + swapped[rows] for rows in parts]
    keeps, own = lax.optimization_barrier((keeps, own))

    ends = []
    for give, keep, (_, _, axes) in zip(gives, keeps, PARTS):
        for stage in range(2):
            keep = keep + flip(give, axes[stage] + "h")
            half = keep.shape[0] // 2
            if stage == 0:
                keep, give = keep[:half], keep[half:]
        ends += [keep, flip(keep[half:], axes[2] + "h")]
    whole = jax.ShapeDtypeStruct(state.shape, F32)
    derivative, again, total = pl.pallas_call(
        derivative_kernel,
        out_shape=(whole, whole, jax.ShapeDtypeStruct((devices, 1, n), F32)),
        in_specs=[vmem] * 7,
        out_specs=(vmem,) * 3,
        compiler_params=params(8),
    )(own, *ends)
    totals = lax.all_to_all(total, ALL, split_axis=0, concat_axis=0, tiled=True)
    advanced = pl.pallas_call(
        advance_kernel,
        out_shape=whole,
        in_specs=[smem] + [vmem] * 3,
        out_specs=vmem,
        compiler_params=params(8),
    )(step, totals, again, state)
    return derivative, advanced


def solution(mesh):
    torus = Mesh(mesh.devices.reshape((2,) * 7), ALL)
    whole = P(ALL, None, None, None)
    index = P(ALL, None)
    in_specs = (whole, P(), P(), P(), P(), index, P(ALL, None, None), index, index, P())
    return jax.shard_map(body, mesh=torus, in_specs=in_specs, out_specs=(whole, whole), check_vma=False)
```

```python
import functools

import jax
import jax.numpy as jnp
import numpy as np
from jax import lax
from jax.experimental import pallas as pl
from jax.experimental.pallas import tpu as pltpu
from jax.sharding import Mesh
from jax.sharding import PartitionSpec as P

ALL = ("xh", "xl", "c", "yh", "yl", "zh", "zl")
UNROLL = 6
F32 = jnp.float32
BF16 = jnp.bfloat16
PARTS = ((0, 3, "xyz"), (3, 6, "yzx"), (6, 8, "zxy"))


def dot(a, b):
    return jnp.dot(a, b, preferred_element_type=F32)


def cell_pairs(axis):
    pairs = []
    for x, c, y, z in np.ndindex(4, 2, 4, 4):
        at = {"x": x, "y": y, "z": z}
        to = dict(at)
        to[axis] = (((at[axis] + c) % 4 ^ 1) - c) % 4
        pairs.append((((x * 2 + c) * 4 + y) * 4 + z, ((to["x"] * 2 + c) * 4 + to["y"]) * 4 + to["z"]))
    return pairs


def flip(value, axis):
    return lax.ppermute(value, axis, [(0, 1), (1, 0)])


def split(value):
    high = value.astype(BF16)
    return high, (value - high.astype(F32)).astype(BF16)


def load_modes(q_ref, left_ref, right_ref):
    n = q_ref.shape[-1]

    def one(k, carry):
        high, low = split(q_ref[k])
        left_ref[k, :n, :n] = high
        left_ref[k, :n, n:] = high
        left_ref[k, n:, :n] = low
        left_ref[k, n:, n:] = low
        right_ref[k, :n, :n] = high
        right_ref[k, :n, n:] = low
        right_ref[k, n:, :n] = high
        right_ref[k, n:, n:] = low
        return carry

    lax.fori_loop(0, q_ref.shape[0], one, 0)


def products(left, right, u):
    n = u.shape[-1]
    high, low = split(u)
    tall = jnp.concatenate(
        [jnp.concatenate([high[0], high[1]], axis=1), jnp.concatenate([low[0], low[1]], axis=1)], axis=0
    )
    z = dot(left, tall)
    z = z[:n] + z[n:]
    wide = jnp.concatenate([high.reshape(2 * n, n), low.reshape(2 * n, n)], axis=1)
    w = dot(wide, right)
    w = w[:, :n] + w[:, n:]
    return z[:, :n], z[:, n:], w[:n], w[n:]


def plan_kernel(at_ref, low_ref, high_ref, lists_ref, plan_ref):
    x, y, z, c = (at_ref[i] for i in range(4))
    table = jnp.concatenate([low_ref[...], high_ref[...]], axis=0)
    row = lax.broadcasted_iota(jnp.int32, table.shape, 0) >> 3
    lane = lax.broadcasted_iota(jnp.int32, table.shape, 1)
    dx, dy, dz = x ^ (row & 2), y ^ ((row & 4) >> 1), z ^ ((row & 8) >> 2)
    device = (((dx << 1) + (c ^ (row & 1)) << 2) + dy << 2) + dz
    chosen = jnp.where(lane == device, 1.0, 0.0)
    listed = lax.dot_general(
        chosen, lists_ref[...], (((1,), (1,)), ((), ())), preferred_element_type=F32
    )
    far = table - 8
    owner = {"x": far >> 5, "y": (far >> 2) & 3, "z": far & 3}
    inside = (far >= 0) & (((far >> 4) & 1) == c) & (lane < 32)
    differs = {}
    for a, ours in zip("xyz", (x, y, z)):
        theirs, ours = (owner[a] + c) & 3, (ours + c) & 3
        inside = inside & ((theirs >> 1) == (ours >> 1))
        differs[a] = (theirs ^ ours) & 1
    member = sum(differs[a] << s for s, a in enumerate(PARTS[2][2]))
    slot = jnp.full(table.shape, -1.0, F32)
    for b in range(8):
        slot = jnp.where(member == b, listed[:, b : b + 1], slot)
    slot = slot.astype(jnp.int32)
    position = jnp.zeros(table.shape, jnp.int32)
    for lo, hi, order in PARTS:
        block = sum(differs[a] << s for s, a in enumerate(order))
        place = 8 * lo + block * (hi - lo) + slot - lo + ((block >> 2) << 6)
        position = jnp.where((slot >= lo) & (slot < hi), place, position)
    valid = inside & (slot >= 0)
    power = (1 << (lane & 15)).astype(F32)

    def half(bits):
        return jnp.sum(jnp.where(bits, power, 0.0), axis=1, keepdims=True).astype(jnp.int32)

    mask = half(valid & (lane < 16)) + (half(valid & (lane >= 16)) << 16)
    plan_ref[...] = jnp.where(lane == 48, mask, jnp.where(valid, position, table))


def encode(target, row, slot, source):
    return (((target << 7) + row << 5) + slot << 6) + source


def list_near(table_ref, list_ref):
    def visit(i, count):
        row, slot = i >> 5, i & 31
        entry = table_ref[row, slot]
        list_ref[count] = encode(row, row, slot, entry & 63)
        return count + ((entry >= 0) & (entry < 8)).astype(jnp.int32)

    return pad_list(list_ref, lax.fori_loop(0, 8 * 32, visit, jnp.int32(0), unroll=8))


def list_far(targets, rows_ref, first, plan_ref, list_ref):
    def append(state, target, row):
        bits, count = state
        slot = 31 - lax.clz(bits & -bits)
        list_ref[count] = encode(target, row, slot, plan_ref[row, slot] & 63)
        return bits & (bits - 1), count + 1

    def visit(target, count):
        row = rows_ref[first + target]
        add = functools.partial(append, target=target, row=row)
        return lax.while_loop(lambda s: s[0] != 0, add, (plan_ref[row, 48], count))[1]

    return pad_list(list_ref, lax.fori_loop(0, targets, visit, jnp.int32(0)))


def list_split(targets, rows_ref, plan_ref, early_ref, late_ref):
    def append(state, target, row):
        bits, early, late = state
        slot = 31 - lax.clz(bits & -bits)
        value = plan_ref[row, slot]
        code = encode(target, row, slot, value & 63)
        early_ref[early] = code
        late_ref[late] = code
        return bits & (bits - 1), early + 1 - (value >> 6), late + (value >> 6)

    def visit(target, counts):
        row = rows_ref[target]
        add = functools.partial(append, target=target, row=row)
        return lax.while_loop(lambda s: s[0] != 0, add, (plan_ref[row, 48], *counts))[1:]

    early, late = lax.fori_loop(0, targets, visit, (jnp.int32(0), jnp.int32(0)))
    return pad_list(early_ref, early), pad_list(late_ref, late)


def pad_list(list_ref, count):
    for j in range(UNROLL):
        list_ref[count + j] = 0
    return count


def add_terms(count, list_ref, plan_ref, coef_ref, source_ref, left_ref, right_ref, out_ref):
    modes = coef_ref.shape[0] // 2

    def step(i, carry):
        for j in range(UNROLL):
            t = i * UNROLL + j
            code = list_ref[t]
            slot = (code >> 6) & 31
            row = (code >> 11) & 127
            target = code >> 18
            k = slot & (modes - 1)
            weight = plan_ref[row, 2 * modes + k].astype(F32)
            down = slot >= modes
            live = t < count
            alpha = jnp.where(live, jnp.where(down, weight * coef_ref[k], 1.0), 0.0)
            beta = jnp.where(live & down, weight * coef_ref[modes + k], 0.0)
            a_re, a_im, b_re, b_im = products(left_ref[k], right_ref[k], source_ref[code & 63])
            out_ref[target, 0] += alpha * (a_im - b_im) + beta * (a_re + b_re)
            out_ref[target, 1] += beta * (a_im + b_im) - alpha * (a_re - b_re)
        return carry

    lax.fori_loop(0, (count + UNROLL - 1) // UNROLL, step, 0)


def own_kernel(
    table_ref, coef_ref, rate_ref, source_ref, left_ref, right_ref, h_ref, out_ref, hl_ref, hr_ref, list_ref
):
    load_modes(h_ref, hl_ref, hr_ref)
    modes = left_ref.shape[0]

    def one(m, carry):
        u = source_ref[m]
        damp = jnp.float32(0)
        for k in range(modes):
            damp += table_ref[m, 2 * modes + k].astype(F32) * rate_ref[k]
        ra, ia, rb, ib = products(hl_ref[0], hr_ref[0], u)
        rc, ic, rd, im = products(hl_ref[1], hr_ref[1], u)
        comm_re = (ra - ic) - (rb - im)
        comm_im = (ia + rc) - (ib + rd)
        out_ref[m, 0] = comm_im - damp * u[0]
        out_ref[m, 1] = -comm_re - damp * u[1]
        return carry

    lax.fori_loop(0, source_ref.shape[0], one, 0)
    count = list_near(table_ref, list_ref)
    add_terms(count, list_ref, table_ref, coef_ref, source_ref, left_ref, right_ref, out_ref)


HELD = ((0, 1), (1, 1), (2, 2), (4, 4))


def clear(out_ref):
    def one(m, carry):
        out_ref[m] = jnp.zeros(out_ref.shape[1:], F32)
        return carry

    lax.fori_loop(0, out_ref.shape[0], one, 0)


def block_copies(blocks, stages, source_ref, sems):
    copies = []
    for (lo, hi, _), part in zip(PARTS, blocks):
        size = hi - lo
        for block, (first, members) in zip(part, (HELD[i] for i in stages)):
            for b in range(members):
                src = block.at[pl.ds(b * (block.shape[0] // members), size)]
                copies.append((src, source_ref.at[pl.ds(8 * lo + (first + b) * size, size)]))
    return [pltpu.make_async_copy(a, b, sems.at[i]) for i, (a, b) in enumerate(copies)]


def early_kernel(q_ref, *refs):
    blocks, (source_ref, left_ref, right_ref, sems) = refs[:-4], refs[-4:]
    own = [blocks[0].at[pl.ds(lo, hi - lo)] for lo, hi, _ in PARTS]
    parts = [[own[i], *blocks[1 + 2 * i : 3 + 2 * i]] for i in range(len(PARTS))]
    copies = block_copies(parts, (0, 1, 2), source_ref, sems)
    for copy in copies:
        copy.start()
    load_modes(q_ref, left_ref, right_ref)
    for copy in copies:
        copy.wait()


def first_kernel(
    plan_ref, coef_ref, rows_ref, left_ref, right_ref, _, a_ref, b_ref, c_ref, source_ref, out_ref, *refs
):
    early_ref, late_ref, sems = refs
    copies = block_copies([[a_ref], [b_ref], [c_ref]], (3,), source_ref, sems)
    for copy in copies:
        copy.start()
    early, late = list_split(out_ref.shape[0], rows_ref, plan_ref, early_ref, late_ref)
    clear(out_ref)
    add_terms(early, early_ref, plan_ref, coef_ref, source_ref, left_ref, right_ref, out_ref)
    for copy in copies:
        copy.wait()
    add_terms(late, late_ref, plan_ref, coef_ref, source_ref, left_ref, right_ref, out_ref)


def next_kernel(outs, plan_ref, coef_ref, rows_ref, source_ref, left_ref, right_ref, *refs):
    list_ref = refs[outs]
    for i, out_ref in enumerate(refs[:outs]):
        targets = out_ref.shape[0]
        count = list_far(targets, rows_ref, i * targets, plan_ref, list_ref)
        clear(out_ref)
        add_terms(count, list_ref, plan_ref, coef_ref, source_ref, left_ref, right_ref, out_ref)


def derivative_kernel(own_ref, *refs):
    ins, (out_ref, again_ref, total_ref) = refs[:-3], refs[-3:]
    squares = jnp.zeros(own_ref.shape[2:], F32)
    for i, (lo, hi, _) in enumerate(PARTS):
        keep_ref, mate_ref = ins[2 * i : 2 * i + 2]
        for m in range(lo, hi):
            for part in range(2):
                value = own_ref[m, part] + (keep_ref[m - lo, part] + mate_ref[m - lo, part])
                out_ref[m, part] = value
                again_ref[m, part] = value
                squares += value * value
    total = jnp.sum(jnp.sum(squares, axis=0, keepdims=True), axis=1, keepdims=True)
    total_ref[...] = jnp.broadcast_to(total.reshape(1, 1, 1), total_ref.shape)


def advance_kernel(step_ref, totals_ref, derivative_ref, state_ref, out_ref):
    total = jnp.sum(totals_ref[...], axis=0)
    rms = jnp.sqrt(total / (totals_ref.shape[0] * derivative_ref.size) + 1e-06)
    scale = step_ref[0] / rms
    for m in range(out_ref.shape[0]):
        for part in range(2):
            out_ref[m, part] = state_ref[m, part] + scale * derivative_ref[m, part]


def spec(space):
    return pl.BlockSpec(memory_space=space)


def params(mib):
    return pltpu.CompilerParams(vmem_limit_bytes=mib << 20)


def mode_scratch(modes, n):
    return [pltpu.VMEM((modes, 2 * n, 2 * n), BF16)] * 2


def cost(terms, n):
    return pl.CostEstimate(flops=terms * 4 * (2 * n) ** 3, bytes_accessed=1 << 23, transcendentals=0)


def served_rows(rc, high):
    rows = []
    for lo, hi, order in PARTS:
        weight = ["xyz".index(a) for a in order]
        for second, third in np.ndindex(2, 2):
            b = 2 * ((high << weight[0]) + (second << weight[1]) + (third << weight[2])) + rc
            rows += [b * 8 + m for m in range(lo, hi)]
    return np.array(rows, np.int32)


def body(
    state,
    hamiltonian,
    couplings,
    bath_coef,
    bath_rate,
    occupation,
    send_list,
    up_index,
    down_index,
    step,
):
    local, _, n, _ = state.shape
    modes = couplings.shape[0]
    devices = send_list.shape[1]
    bit = {a: lax.axis_index(a) for a in ALL}
    at = jnp.stack([2 * bit[a + "h"] + bit[a + "l"] for a in "xyz"] + [bit["c"]]).astype(jnp.int32)
    pairs = {a: cell_pairs(a) for a in "xyz"}

    held = [[state[lo:hi]] for lo, hi, _ in PARTS]
    note = jnp.zeros((1, 2, n, n), F32).at[0, 0, 0, :devices].set(send_list.reshape(devices).astype(F32))
    held[2][0] = jnp.concatenate([held[2][0], note], axis=0)
    table = jnp.concatenate(
        [up_index, down_index, occupation, jnp.zeros((local, devices - 3 * modes), jnp.int32)], axis=1
    )
    tables = jnp.concatenate([table, flip(table, "c")], axis=0)
    for stage in range(3):
        sends = [part[0] if stage == 0 else jnp.concatenate(part, axis=0) for part in held]
        sends, tables = lax.optimization_barrier((sends, tables))
        for part, block, (_, _, order) in zip(held, sends, PARTS):
            part.append(lax.ppermute(block, ALL, pairs[order[stage]]))
        other = flip(tables, "xyz"[stage] + "h")
        if stage < 2:
            tables = jnp.concatenate([tables, other], axis=0)
    lists = jnp.concatenate([block[2::3, 0, 0, :devices] for block in held[2]], axis=0)

    smem, vmem = spec(pltpu.SMEM), spec(pltpu.VMEM)
    plan = pl.pallas_call(
        plan_kernel,
        out_shape=jax.ShapeDtypeStruct((2 * tables.shape[0], devices), jnp.int32),
        in_specs=[smem] + [vmem] * 3,
        out_specs=vmem,
        compiler_params=params(4),
    )(at, tables, other, lists)

    coef = bath_coef.reshape(-1)
    listing = pltpu.SMEM((1024 + UNROLL,), jnp.int32)
    target = jax.ShapeDtypeStruct((4 * local, 2, n, n), F32)
    half_modes = jax.ShapeDtypeStruct((modes, 2 * n, 2 * n), BF16)

    everything = jax.ShapeDtypeStruct((8 * local, 2, n, n), F32)
    early, late = [state], []
    for part in held:
        early += part[1:3]
        late.append(part[3])
    early, _ = lax.optimization_barrier((early, sends))
    early, late = ([pltpu.with_memory_space_constraint(b, pltpu.HBM) for b in group] for group in (early, late))
    source, left, right = pl.pallas_call(
        early_kernel,
        out_shape=(everything, half_modes, half_modes),
        in_specs=[vmem] + [spec(pltpu.HBM)] * len(early),
        out_specs=(vmem,) * 3,
        scratch_shapes=[pltpu.SemaphoreType.DMA((12,))],
        compiler_params=params(20),
        cost_estimate=cost(160, n),
    )(couplings, *early)

    source, other = pl.pallas_call(
        first_kernel,
        out_shape=(everything, target),
        in_specs=[smem] * 3 + [vmem] * 3 + [spec(pltpu.HBM)] * 3,
        out_specs=(vmem,) * 2,
        scratch_shapes=[listing, listing, pltpu.SemaphoreType.DMA((12,))],
        input_output_aliases={5: 0},
        compiler_params=params(24),
        cost_estimate=cost(32, n),
    )(plan, coef, served_rows(1, 1), left, right, source, *late)
    parts = [slice(4 * lo, 4 * hi) for lo, hi, _ in PARTS]
    swapped = flip(other, "c")

    def later(plan, rows, outs):
        return pl.pallas_call(
            functools.partial(next_kernel, outs),
            out_shape=(target,) * outs,
            in_specs=[smem] * 3 + [vmem] * 3,
            out_specs=(vmem,) * outs,
            scratch_shapes=[listing],
            compiler_params=params(24),
            cost_estimate=cost(24 * outs, n),
        )(plan, coef, rows, source, left, right)

    same, other = later(plan, np.concatenate([served_rows(0, 1), served_rows(1, 0)]), 2)
    gives = [same[rows] + swapped[rows] for rows in parts]

    here, plan, gives, other = lax.optimization_barrier((state, plan, gives, other))
    swapped = flip(other, "c")
    own = pl.pallas_call(
        own_kernel,
        out_shape=jax.ShapeDtypeStruct(state.shape, F32),
        in_specs=[smem] * 3 + [vmem] * 4,
        out_specs=vmem,
        scratch_shapes=mode_scratch(2, n) + [listing],
        compiler_params=params(16),
        cost_estimate=cost(160, n),
    )(table, coef, bath_rate, here, left, right, hamiltonian)
    (kept,) = later(plan, served_rows(0, 0), 1)
    keeps = [kept[rows] + swapped[rows] for rows in parts]
    keeps, own = lax.optimization_barrier((keeps, own))

    ends = []
    for give, keep, (_, _, axes) in zip(gives, keeps, PARTS):
        for stage in range(2):
            keep = keep + flip(give, axes[stage] + "h")
            half = keep.shape[0] // 2
            if stage == 0:
                keep, give = keep[:half], keep[half:]
        ends += [keep, flip(keep[half:], axes[2] + "h")]
    whole = jax.ShapeDtypeStruct(state.shape, F32)
    derivative, again, total = pl.pallas_call(
        derivative_kernel,
        out_shape=(whole, whole, jax.ShapeDtypeStruct((devices, 1, n), F32)),
        in_specs=[vmem] * 7,
        out_specs=(vmem,) * 3,
        compiler_params=params(8),
    )(own, *ends)
    totals = lax.all_to_all(total, ALL, split_axis=0, concat_axis=0, tiled=True)
    advanced = pl.pallas_call(
        advance_kernel,
        out_shape=whole,
        in_specs=[smem] + [vmem] * 3,
        out_specs=vmem,
        compiler_params=params(8),
    )(step, totals, again, state)
    return derivative, advanced


def solution(mesh):
    torus = Mesh(mesh.devices.reshape((2,) * 7), ALL)
    whole = P(ALL, None, None, None)
    index = P(ALL, None)
    in_specs = (whole, P(), P(), P(), P(), index, P(ALL, None, None), index, index, P())
    return jax.shard_map(body, mesh=torus, in_specs=in_specs, out_specs=(whole, whole), check_vma=False)
```
